32 devices in a mesh: group: 2 (over y), tile: 8 (over z, x), strip: 2 (over core).
Axes of the slice: x: 2, y: 2, z: 4, core: 2. Of those that a mesh axis runs over, the one named last changes fastest.
Arguments:
- image: bfloat16 [128, 256, 256], P(('group', 'strip'), 'tile'), parts along dimension 0, may hold values from -16 to 16
- bn_gain: float32 [256], replicated, may hold values from 0.25 to 1.75
- bn_shift: float32 [256], replicated, may hold values from -3 to 3
- w_expand: bfloat16 [256, 1024], replicated, may hold values from -0.375 to 0.375
- b_expand: float32 [1024], replicated, may hold values from -3 to 3
- w_depth: float32 [9, 1024], replicated, may hold values from -2 to 2
- b_depth: float32 [1024], replicated, may hold values from -3 to 3
- w_project: bfloat16 [1024, 256], replicated, may hold values from -0.1875 to 0.1875
- b_project: float32 [256], replicated, may hold values from -3 to 3
- attn_gain: float32 [256], replicated, may hold values from 0.25 to 1.75
- attn_shift: float32 [256], replicated, may hold values from -2 to 2
- w_qkv: bfloat16 [256, 768], replicated, may hold values from -0.375 to 0.375
- w_out: bfloat16 [256, 256], replicated, may hold values from -0.375 to 0.375
- rel_table: float32 [8, 225], replicated, may hold values from -4 to 304
- ffn_gain: float32 [256], replicated, may hold values from 0.25 to 1.75
- ffn_shift: float32 [256], replicated, may hold values from -2 to 2
- w_up: bfloat16 [256, 1024], replicated, may hold values from -0.375 to 0.375
- b_up: float32 [1024], replicated, may hold values from -3 to 3
- w_down: bfloat16 [1024, 256], replicated, may hold values from -0.1875 to 0.1875
- b_down: float32 [256], replicated, may hold values from -3 to 3
Outputs:
- block_out: bfloat16 [128, 256, 256], P(('group', 'strip'), 'tile'), parts along dimension 0
The draws below stay inside these ranges and needn't reach their ends.
There are 2 independent parts, one for each index of `group`. The reference program is written for one: setup_inputs(seed, part) draws one part's arguments, and reference() takes and returns one part's arrays. A program takes and returns all parts, laid end to end along the dimension named above; an argument that names none is the same for every part. Nothing has to cross between parts.
All inputs are finite; a program needn't handle non-finite values.
Results may differ from the reference program's by a relative error of at most 0.0064.
Values may be sent and summed in bfloat16 or wider, within the bound.
A program may use at most 64 MiB of HBM per device.

```python
import math
import jax
import jax.numpy as jnp
from jax import lax

C = 256
E = 1024
F = 1024
GRID = 8
TW = 32
HEADS = 8
H = 64
W = 256


def draw_image(key, part):
    key_noise = jax.random.fold_in(key, 11)
    key_token = jax.random.fold_in(key, 12)
    key_channel = jax.random.fold_in(key, 13)
    low_log = math.log(0.3)
    high_log = math.log(3.0)
    chan_scale = jnp.exp(jax.random.uniform(key_channel, (C,), jnp.float32, low_log, high_log))
    token_scale = jnp.exp(jax.random.uniform(key_token, (H, W, 1), jnp.float32, low_log, high_log))
    noise = jax.random.normal(key_noise, (H, W, C), jnp.float32)
    pixels = noise * token_scale * chan_scale
    return jnp.clip(pixels, -16.0, 16.0).astype(jnp.bfloat16)


def draw_rel_table(key, part):
    entries = (2 * GRID - 1) ** 2
    key_base = jax.random.fold_in(key, 21)
    base_table = jnp.clip(jax.random.normal(key_base, (HEADS, entries), jnp.float32), -4.0, 4.0)
    return base_table.astype(jnp.float32)


def gaussian(own_key, dims, scale, limit, held_as=jnp.bfloat16):
    return jnp.clip(scale * jax.random.normal(own_key, dims, jnp.float32), -limit, limit).astype(held_as)


def setup_inputs(seed: int = 0, part: int = 0) -> dict:
    keys = jax.random.split(jax.random.key(seed), 21)
    part_keys = jax.random.split(jax.random.fold_in(keys[20], part), 21)
    return {
        "image": draw_image(jax.random.fold_in(jax.random.fold_in(keys[20], part), 71), part),
        "bn_gain": jnp.clip(1.0 + 0.15 * jax.random.normal(keys[1], (C,), jnp.float32), 0.25, 1.75),
        "bn_shift": gaussian(keys[2], (C,), 0.5, 3.0, jnp.float32),
        "w_expand": gaussian(keys[3], (C, E), C ** -0.5, 0.375),
        "b_expand": gaussian(keys[4], (E,), 0.5, 3.0, jnp.float32),
        "w_depth": gaussian(keys[5], (9, E), 9 ** -0.5, 2.0, jnp.float32),
        "b_depth": gaussian(keys[6], (E,), 0.5, 3.0, jnp.float32),
        "w_project": gaussian(keys[7], (E, C), E ** -0.5, 0.1875),
        "b_project": gaussian(keys[8], (C,), 0.5, 3.0, jnp.float32),
        "attn_gain": jnp.clip(1.0 + 0.15 * jax.random.normal(keys[9], (C,), jnp.float32), 0.25, 1.75),
        "attn_shift": gaussian(keys[10], (C,), 0.3, 2.0, jnp.float32),
        "w_qkv": gaussian(keys[11], (C, 3 * C), C ** -0.5, 0.375),
        "w_out": gaussian(keys[12], (C, C), C ** -0.5, 0.375),
        "rel_table": draw_rel_table(jax.random.fold_in(keys[20], 71), part),
        "ffn_gain": jnp.clip(1.0 + 0.15 * jax.random.normal(keys[14], (C,), jnp.float32), 0.25, 1.75),
        "ffn_shift": gaussian(keys[15], (C,), 0.3, 2.0, jnp.float32),
        "w_up": gaussian(keys[16], (C, F), C ** -0.5, 0.375),
        "b_up": gaussian(keys[17], (F,), 0.5, 3.0, jnp.float32),
        "w_down": gaussian(keys[18], (F, C), F ** -0.5, 0.1875),
        "b_down": gaussian(keys[19], (C,), 0.5, 3.0, jnp.float32),
    }


EPSILON = 1e-05

def gelu_tanh(inputs):
    return jax.nn.gelu(inputs, approximate=True)

def layer_norm(inputs, norm_gain, norm_shift):
    center = lax.optimization_barrier(jnp.mean(inputs, axis=-1, keepdims=True))
    spread = lax.optimization_barrier(jnp.mean(jnp.square(inputs - center), axis=-1, keepdims=True))
    return (inputs - center) * lax.rsqrt(spread + EPSILON) * norm_gain + norm_shift

def expand_tokens(pixels, bn_gain, bn_shift, w_expand, b_expand):
    normed = (pixels.astype(jnp.float32) * bn_gain + bn_shift).astype(jnp.bfloat16)
    pre_act = jnp.dot(normed, w_expand, preferred_element_type=jnp.float32) + b_expand
    return gelu_tanh(pre_act).astype(jnp.bfloat16)

def depthwise(framed, w_depth, b_depth):
    out_rows = framed.shape[0] - 2
    out_cols = framed.shape[1] - 2
    accum_sum = jnp.zeros((out_rows, out_cols, framed.shape[2]), jnp.float32) + b_depth
    for row_step in range(3):
        for col_step in range(3):
            window_part = framed[row_step:row_step + out_rows, col_step:col_step + out_cols]
            accum_sum = accum_sum + window_part.astype(jnp.float32) * w_depth[row_step * 3 + col_step]
    return gelu_tanh(accum_sum).astype(jnp.bfloat16)

def position_bias(rel_table):
    grid_side = GRID
    token_ids = jnp.arange(grid_side * grid_side, dtype=jnp.int32)
    row_of = token_ids // grid_side
    col_of = token_ids % grid_side
    offset = (row_of[:, None] - row_of[None, :] + grid_side - 1) * (2 * grid_side - 1) + (col_of[:, None] - col_of[None, :] + grid_side - 1)
    entry_ids = jnp.arange((2 * grid_side - 1) ** 2, dtype=jnp.int32)
    onehot = (offset.reshape(-1)[:, None] == entry_ids[None, :]).astype(jnp.float32)
    pos_bias = jnp.dot(rel_table, onehot.T, precision=lax.Precision.HIGHEST, preferred_element_type=jnp.float32)
    return pos_bias.reshape(rel_table.shape[0], grid_side * grid_side, grid_side * grid_side)

def grid_attention(windows, attn_gain, attn_shift, w_qkv, w_out, pos_bias):
    win_count = windows.shape[0]
    places = windows.shape[1]
    model_width = windows.shape[2]
    head_count = pos_bias.shape[0]
    head_size = model_width // head_count
    normed = layer_norm(windows.astype(jnp.float32), attn_gain, attn_shift).astype(jnp.bfloat16)
    projected_qkv = jnp.dot(normed, w_qkv, preferred_element_type=jnp.float32)
    queries = (projected_qkv[..., :model_width] * head_size ** (-0.5)).astype(jnp.bfloat16)
    key_heads = projected_qkv[..., model_width:2 * model_width].astype(jnp.bfloat16)
    value_heads = projected_qkv[..., 2 * model_width:].astype(jnp.bfloat16)
    queries = queries.reshape(win_count, places, head_count, head_size).astype(jnp.float32)
    key_heads = key_heads.reshape(win_count, places, head_count, head_size).astype(jnp.float32)
    value_heads = value_heads.reshape(win_count, places, head_count, head_size).astype(jnp.float32)
    scores = jnp.einsum('wihd,wjhd->whij', queries, key_heads, precision=lax.Precision.HIGHEST) + pos_bias[None]
    row_peak = lax.optimization_barrier(jnp.max(scores, axis=-1, keepdims=True))
    exp_scores = jnp.exp(scores - row_peak)
    weights_bf = (exp_scores / lax.optimization_barrier(jnp.sum(exp_scores, axis=-1, keepdims=True))).astype(jnp.bfloat16)
    context = jnp.einsum('whij,wjhd->wihd', weights_bf.astype(jnp.float32), value_heads, precision=lax.Precision.HIGHEST)
    context = context.astype(jnp.bfloat16).reshape(win_count, places, model_width)
    attended = windows.astype(jnp.float32) + jnp.dot(context, w_out, preferred_element_type=jnp.float32)
    return attended.astype(jnp.bfloat16)

def feed_forward(tokens_in, ffn_gain, ffn_shift, w_up, b_up, w_down, b_down):
    normed = layer_norm(tokens_in.astype(jnp.float32), ffn_gain, ffn_shift).astype(jnp.bfloat16)
    hidden = gelu_tanh(jnp.dot(normed, w_up, preferred_element_type=jnp.float32) + b_up).astype(jnp.bfloat16)
    result = tokens_in.astype(jnp.float32) + jnp.dot(hidden, w_down, preferred_element_type=jnp.float32) + b_down
    return result.astype(jnp.bfloat16)

def reference(image, bn_gain, bn_shift, w_expand, b_expand, w_depth, b_depth, w_project, b_project, attn_gain, attn_shift, w_qkv, w_out, rel_table, ffn_gain, ffn_shift, w_up, b_up, w_down, b_down):
    height = image.shape[0]
    width_all = image.shape[1]
    channels = image.shape[2]
    blocks = width_all // TW
    padded = jnp.pad(image, ((0, 0), (1, 1), (0, 0)))

    def column_block(block_at):
        start_col = (block_at * TW).astype(jnp.int32)
        window_cols = lax.dynamic_slice_in_dim(padded, start_col, TW + 2, 1)
        expanded = expand_tokens(window_cols, bn_gain, bn_shift, w_expand, b_expand)
        col_index = start_col - 1 + jnp.arange(TW + 2, dtype=jnp.int32)
        inside = (col_index >= 0) & (col_index < width_all)
        expanded = jnp.where(inside[None, :, None], expanded, jnp.zeros((), jnp.bfloat16))
        expanded = jnp.pad(expanded, ((1, 1), (0, 0), (0, 0)))
        hidden = depthwise(expanded, w_depth, b_depth)
        projected = jnp.dot(hidden, w_project, preferred_element_type=jnp.float32) + b_project
        return (window_cols[:, 1:-1].astype(jnp.float32) + projected).astype(jnp.bfloat16)
    section_one = lax.map(column_block, jnp.arange(blocks, dtype=jnp.int32))
    section_one = section_one.transpose(1, 0, 2, 3).reshape(height, width_all, channels)
    across = height // GRID
    along_cols = width_all // GRID
    windows = section_one.reshape(GRID, across, GRID, along_cols, channels).transpose(1, 3, 0, 2, 4)
    total_windows = across * along_cols
    windows = windows.reshape(total_windows, GRID * GRID, channels)
    pos_bias = position_bias(rel_table)
    per_block = math.gcd(total_windows, 64)
    grouped = windows.reshape(total_windows // per_block, per_block, GRID * GRID, channels)

    def window_block(window_group):
        attended = grid_attention(window_group, attn_gain, attn_shift, w_qkv, w_out, pos_bias)
        return feed_forward(attended, ffn_gain, ffn_shift, w_up, b_up, w_down, b_down)
    result = lax.map(window_block, grouped)
    result = result.reshape(across, along_cols, GRID, GRID, channels).transpose(2, 0, 3, 1, 4)
    return result.reshape(height, width_all, channels)
```

```python
import functools

import jax
import jax.numpy as jnp
from jax import lax
from jax.experimental import pallas as pl
from jax.experimental.pallas import tpu as pltpu
from jax.sharding import PartitionSpec as P

GRID = 8
EPSILON = 1e-05
MESH = pl.DeviceIdType.MESH


def padded(value, sides, width):
    for axis, dim in sides:
        devices, length = (lax.axis_size(axis), value.shape[dim])
        up = [(i, (i + 1) % devices) for i in range(devices - 1)]
        down = [(j, i) for i, j in up]
        last = lax.slice_in_dim(value, length - width, length, axis=dim)
        initial = lax.slice_in_dim(value, 0, width, axis=dim)
        before = lax.ppermute(last, axis, up)
        after = lax.ppermute(initial, axis, down)
        value = jnp.concatenate([before, value, after], axis=dim)
    return value


def gelu_tanh(inputs):
    return jax.nn.gelu(inputs, approximate=True)


def layer_norm(inputs, norm_gain, norm_shift):
    center = jnp.mean(inputs, axis=-1, keepdims=True)
    spread = jnp.mean(jnp.square(inputs - center), axis=-1, keepdims=True)
    return (inputs - center) * lax.rsqrt(spread + EPSILON) * norm_gain + norm_shift


def expand_tokens(pixels, bn_gain, bn_shift, w_expand, b_expand):
    normed = (pixels.astype(jnp.float32) * bn_gain + bn_shift).astype(jnp.bfloat16)
    pre_act = jnp.dot(normed, w_expand, preferred_element_type=jnp.float32) + b_expand
    return gelu_tanh(pre_act).astype(jnp.bfloat16)


def depthwise(framed, w_depth, b_depth):
    out_rows = framed.shape[0] - 2
    out_cols = framed.shape[1] - 2
    accum_sum = jnp.zeros((out_rows, out_cols, framed.shape[2]), jnp.float32) + b_depth
    for row_step in range(3):
        for col_step in range(3):
            window_part = framed[row_step : row_step + out_rows, col_step : col_step + out_cols]
            accum_sum = (
                accum_sum + window_part.astype(jnp.float32) * w_depth[row_step * 3 + col_step]
            )
    return gelu_tanh(accum_sum).astype(jnp.bfloat16)


def place_bias(rel_table, piece):
    heads = rel_table.shape[0]
    side = 2 * GRID - 1
    table = rel_table.reshape(heads, side, side)
    by_row = jnp.stack(
        [table[:, GRID - 1 - k : 2 * GRID - 1 - k, :] for k in range(GRID)]
    )
    by_col = jnp.stack(
        [by_row[..., GRID - 1 - k : 2 * GRID - 1 - k] for k in range(GRID)], axis=1
    )
    rows = piece // GRID
    by_col = by_col.reshape(GRID * GRID, heads, GRID // rows, rows * GRID)
    return by_col.transpose(2, 0, 1, 3).reshape(GRID // rows, GRID * GRID, heads * piece)


def dot(a, b):
    return jnp.dot(a, b, preferred_element_type=jnp.float32)


def back_kernel(
    strips,
    col_groups,
    head_count,
    sec_ref,
    ag_ref,
    as_ref,
    wqkv_ref,
    wout_ref,
    bias_ref,
    fg_ref,
    fs_ref,
    wup_ref,
    bup_ref,
    wdown_ref,
    bdown_ref,
    out_ref,
    arr,
    q_s,
    k_s,
    v_s,
    ctx_s,
    outb,
    sec2,
    send1,
    recv1,
    send2,
    recv2,
):
    grid_rows, _, cols, chans = sec_ref.shape
    part = cols // strips
    piece = ctx_s.shape[1]
    blocks = GRID * GRID // piece
    per_block = piece // GRID
    head_size = chans // head_count
    me_s = lax.axis_index("strip")
    tile = lax.axis_index("tile")
    me_k = tile // col_groups
    within = tile % col_groups
    peers = strips * GRID

    def device(s, k):
        return {"strip": s, "tile": k * col_groups + within}

    def is_me(s, k):
        return jnp.logical_and(s == me_s, k == me_k)

    barrier = pltpu.get_barrier_semaphore()
    for m in range(1, peers):
        s, k = (me_s + m // GRID) % strips, (me_k + m) % GRID
        pl.semaphore_signal(barrier, inc=1, device_id=device(s, k), device_id_type=MESH)
    pl.semaphore_wait(barrier, peers - 1)

    def first_copy(m):
        s, k = (me_s + m // GRID) % strips, (me_k + m) % GRID
        src = sec_ref.at[:, k, pl.ds(part * s, part)]
        dst = arr.at[pl.ds(grid_rows * me_s, grid_rows), me_k]
        if m == 0:
            return pltpu.make_async_copy(src, dst, recv1.at[me_s, me_k])
        return pltpu.make_async_remote_copy(
            src, dst, send1.at[m], recv1.at[me_s, me_k], device_id=device(s, k), device_id_type=MESH
        )

    for m in list(range(1, peers)) + [0]:
        first_copy(m).start()

    def wait_first(s, k):
        piece_ref = arr.at[pl.ds(grid_rows * s, grid_rows), k]
        pltpu.make_async_copy(piece_ref, piece_ref, recv1.at[s, k]).wait()

    span = piece * part
    row_id = lax.broadcasted_iota(jnp.int32, (span, span), 0)
    col_id = lax.broadcasted_iota(jnp.int32, (span, span), 1)
    swap = jnp.where(col_id == (row_id % piece) * part + row_id // piece, 1.0, 0.0).astype(
        jnp.bfloat16
    )
    lane_head = lax.broadcasted_iota(jnp.int32, (head_count * piece, chans), 1) // head_size
    row_head = lax.broadcasted_iota(jnp.int32, (head_count * piece, chans), 0) // piece
    mask = jnp.where(lane_head == row_head, 1.0, 0.0)
    mask_bf = mask.astype(jnp.bfloat16)

    blocks_per_strip = blocks // strips
    for b in range(blocks):
        if b % blocks_per_strip == 0:
            for k in range(GRID):
                wait_first(b // blocks_per_strip, k)
        x = arr[per_block * b : per_block * (b + 1)].reshape(span, chans).astype(jnp.float32)
        normed = layer_norm(x, ag_ref[...], as_ref[...]).astype(jnp.bfloat16)
        normed = dot(swap, normed).astype(jnp.bfloat16)
        qkv = dot(normed, wqkv_ref[...])
        q = (qkv[:, :chans] * head_size ** (-0.5)).astype(jnp.bfloat16)
        q_s[b] = q.reshape(part, piece, chans)
        k_s[:, piece * b : piece * (b + 1), :] = (
            qkv[:, chans : 2 * chans].astype(jnp.bfloat16).reshape(part, piece, chans)
        )
        v_s[:, piece * b : piece * (b + 1), :] = (
            qkv[:, 2 * chans :].astype(jnp.bfloat16).reshape(part, piece, chans)
        )

    def back_copy(b, k):
        s = b // blocks_per_strip
        half = b % blocks_per_strip
        src = outb.at[pl.ds(per_block * b, per_block), k]
        dst = sec2.at[pl.ds(per_block * half, per_block), me_k, pl.ds(part * me_s, part)]
        remote = pltpu.make_async_remote_copy(
            src,
            dst,
            send2.at[b, k],
            recv2.at[half, me_s, me_k],
            device_id=device(s, k),
            device_id_type=MESH,
        )
        own = pltpu.make_async_copy(src, dst, recv2.at[half, me_s, me_k])
        return s, remote, own

    for b in range(blocks):
        for w in range(part):
            q16 = q_s[b, w]
            qbd = jnp.concatenate([q16] * head_count, axis=0) * mask_bf
            s = lax.dot_general(
                k_s[w], qbd, (((1,), (1,)), ((), ())), preferred_element_type=jnp.float32
            )
            s = s + bias_ref[b]
            e = jnp.exp(s - jnp.max(s, axis=0, keepdims=True))
            p = (e * (1.0 / jnp.sum(e, axis=0, keepdims=True))).astype(jnp.bfloat16)
            o = lax.dot_general(
                p, v_s[w], (((0,), (0,)), ((), ())), preferred_element_type=jnp.float32
            )
            o = (o * mask).reshape(head_count, piece, chans)
            ctx_s[w] = jnp.sum(o, axis=0).astype(jnp.bfloat16)
        ctx = dot(swap, ctx_s[...].reshape(span, chans)).astype(jnp.bfloat16)
        x = arr[per_block * b : per_block * (b + 1)].reshape(span, chans).astype(jnp.float32)
        attended = (x + dot(ctx, wout_ref[...])).astype(jnp.bfloat16)
        outb[per_block * b : per_block * (b + 1)] = attended.reshape(per_block, GRID, part, chans)
        for m in range(GRID):
            k = (me_k + m) % GRID
            s, remote, own = back_copy(b, k)

            @pl.when(jnp.logical_not(is_me(s, k)))
            def _():
                remote.start()

            @pl.when(is_me(s, k))
            def _():
                own.start()

    pairs = GRID // 2
    for m in range(pairs):
        pair = (me_k // 2 + m) % pairs
        for s in range(strips):
            for kk in range(2):
                k = 2 * pair + kk
                for half in range(blocks_per_strip):
                    ref = sec2.at[pl.ds(per_block * half, per_block), k, pl.ds(part * s, part)]
                    pltpu.make_async_copy(ref, ref, recv2.at[half, s, k]).wait()
        x = sec2[:, pl.ds(2 * pair, 2)].reshape(grid_rows * 2 * cols, chans).astype(jnp.float32)
        normed = layer_norm(x, fg_ref[...], fs_ref[...]).astype(jnp.bfloat16)
        hidden = gelu_tanh(dot(normed, wup_ref[...]) + bup_ref[...]).astype(jnp.bfloat16)
        res = x + dot(hidden, wdown_ref[...]) + bdown_ref[...]
        out_ref[:, pl.ds(2 * pair, 2)] = res.astype(jnp.bfloat16).reshape(
            grid_rows, 2, cols, chans
        )

    for m in range(1, peers):
        first_copy(m).wait_send()
    for b in range(blocks):
        for k in range(GRID):
            s, remote, own = back_copy(b, k)

            @pl.when(jnp.logical_not(is_me(s, k)))
            def _():
                remote.wait_send()


def local(
    image,
    bn_gain,
    bn_shift,
    w_expand,
    b_expand,
    w_depth,
    b_depth,
    w_project,
    b_project,
    attn_gain,
    attn_shift,
    w_qkv,
    w_out,
    rel_table,
    ffn_gain,
    ffn_shift,
    w_up,
    b_up,
    w_down,
    b_down,
):
    tile_rows, tile_cols, channels = image.shape
    strips = lax.axis_size("strip")
    tile_count = lax.axis_size("tile")
    framed_in = padded(image, (("tile", 1), ("strip", 0)), 1)
    expanded = expand_tokens(framed_in, bn_gain, bn_shift, w_expand, b_expand)
    row_global = (
        lax.axis_index("strip") * tile_rows - 1 + jnp.arange(tile_rows + 2, dtype=jnp.int32)
    )
    col_global = lax.axis_index("tile") * tile_cols - 1 + jnp.arange(tile_cols + 2, dtype=jnp.int32)
    row_ok = (row_global >= 0) & (row_global < tile_rows * strips)
    col_ok = (col_global >= 0) & (col_global < tile_cols * tile_count)
    keep_mask = row_ok[:, None, None] & col_ok[None, :, None]
    framed = jnp.where(keep_mask, expanded, jnp.zeros((), jnp.bfloat16))
    hidden = depthwise(framed, w_depth, b_depth)
    projected = jnp.dot(hidden, w_project, preferred_element_type=jnp.float32) + b_project
    section_one = (image.astype(jnp.float32) + projected).astype(jnp.bfloat16)

    grid_rows = GRID // strips
    across = tile_rows // grid_rows
    col_groups = tile_count // GRID
    heads = rel_table.shape[0]
    part = tile_cols // strips
    piece = part
    blocks = GRID * GRID // piece
    bias = place_bias(rel_table, piece)
    section = section_one.reshape(grid_rows, across, tile_cols, channels)
    bf = jnp.bfloat16
    vmem = pl.BlockSpec(memory_space=pltpu.VMEM)
    out = pl.pallas_call(
        functools.partial(back_kernel, strips, col_groups, heads),
        out_shape=jax.ShapeDtypeStruct(section.shape, bf),
        in_specs=[vmem] * 12,
        out_specs=vmem,
        scratch_shapes=[
            pltpu.VMEM((GRID, GRID, part, channels), bf),
            pltpu.VMEM((blocks, part, piece, channels), bf),
            pltpu.VMEM((part, GRID * GRID, channels), bf),
            pltpu.VMEM((part, GRID * GRID, channels), bf),
            pltpu.VMEM((part, piece, channels), bf),
            pltpu.VMEM((GRID, GRID, part, channels), bf),
            pltpu.VMEM((grid_rows, GRID, tile_cols, channels), bf),
            pltpu.SemaphoreType.DMA((strips * GRID,)),
            pltpu.SemaphoreType.DMA((strips, GRID)),
            pltpu.SemaphoreType.DMA((blocks, GRID)),
            pltpu.SemaphoreType.DMA((blocks // strips, strips, GRID)),
        ],
        compiler_params=pltpu.CompilerParams(collective_id=0, has_side_effects=True),
    )(
        section,
        attn_gain.reshape(1, -1),
        attn_shift.reshape(1, -1),
        w_qkv,
        w_out,
        bias,
        ffn_gain.reshape(1, -1),
        ffn_shift.reshape(1, -1),
        w_up,
        b_up.reshape(1, -1),
        w_down,
        b_down.reshape(1, -1),
    )
    return out.reshape(tile_rows, tile_cols, channels)


def solution(mesh):
    return jax.shard_map(
        local,
        mesh=mesh,
        in_specs=(P(("group", "strip"), "tile", None),) + (P(),) * 19,
        out_specs=P(("group", "strip"), "tile", None),
        check_vma=False,
    )
```

```python
import functools

import jax
import jax.numpy as jnp
from jax import lax
from jax.experimental import pallas as pl
from jax.experimental.pallas import tpu as pltpu
from jax.sharding import PartitionSpec as P

GRID = 8
EPSILON = 1e-05
MESH = pl.DeviceIdType.MESH


def gelu_tanh(inputs):
    return jax.nn.gelu(inputs, approximate=True)


def layer_norm(inputs, norm_gain, norm_shift):
    center = jnp.mean(inputs, axis=-1, keepdims=True)
    spread = jnp.mean(jnp.square(inputs - center), axis=-1, keepdims=True)
    return (inputs - center) * lax.rsqrt(spread + EPSILON) * norm_gain + norm_shift


def place_bias(rel_table):
    heads = rel_table.shape[0]
    side = 2 * GRID - 1
    table = rel_table.reshape(heads, side, side)
    shape = (side, GRID, GRID)
    entry = lax.broadcasted_iota(jnp.int32, shape, 0)
    key = lax.broadcasted_iota(jnp.int32, shape, 1)
    query = lax.broadcasted_iota(jnp.int32, shape, 2)
    onehot = (entry == GRID - 1 + query - key).astype(jnp.float32)
    by_col = jnp.einsum("hde,eki->dkhi", table, onehot, precision=lax.Precision.HIGHEST)
    by_col = by_col.reshape(side, GRID, heads * GRID)
    return jnp.concatenate([by_col[:-1], by_col[1:]], axis=-1)


def dot(a, b):
    return jnp.dot(a, b, preferred_element_type=jnp.float32)


def block_kernel(
    strips,
    col_groups,
    head_count,
    image_ref,
    bng_ref,
    bns_ref,
    wexp_ref,
    bexp_ref,
    wdep_ref,
    bdep_ref,
    wproj_ref,
    bproj_ref,
    ag_ref,
    as_ref,
    wqkv_ref,
    wout_ref,
    bias_ref,
    fg_ref,
    fs_ref,
    wup_ref,
    bup_ref,
    wdown_ref,
    bdown_ref,
    out_ref,
    edge,
    cols_in,
    rows_in,
    rim,
    e_s,
    h_s,
    sec_ref,
    arr,
    q_s,
    k_s,
    v_s,
    ctx_s,
    outb,
    sec2,
    send1,
    recv1,
    send2,
    recv2,
    hsend,
    hrecv,
):
    grid_rows, _, cols, chans = sec_ref.shape
    part = cols // strips
    rows = image_ref.shape[0]
    piece = ctx_s.shape[1]
    blocks = GRID * GRID // piece
    per_block = piece // GRID
    head_size = chans // head_count
    me_s = lax.axis_index("strip")
    tile = lax.axis_index("tile")
    me_k = tile // col_groups
    within = tile % col_groups
    peers = strips * GRID

    def device(s, k):
        return {"strip": s, "tile": k * col_groups + within}

    def is_me(s, k):
        return jnp.logical_and(s == me_s, k == me_k)

    barrier = pltpu.get_barrier_semaphore()
    for m in range(1, peers):
        s, k = (me_s + m // GRID) % strips, (me_k + m) % GRID
        pl.semaphore_signal(barrier, inc=1, device_id=device(s, k), device_id_type=MESH)
    tiles = GRID * col_groups
    sides = ((tile + tiles - 1) % tiles, (tile + 1) % tiles)
    for t in sides:
        for s in range(strips):
            pl.semaphore_signal(
                barrier, inc=1, device_id={"strip": s, "tile": t}, device_id_type=MESH
            )
    pl.semaphore_wait(barrier, peers - 1 + 2 * strips)

    edge[0] = image_ref[:, 0:16, :].astype(jnp.float32)[:, 0, :].astype(jnp.bfloat16)
    edge[1] = image_ref[:, cols - 16 : cols, :].astype(jnp.float32)[:, 15, :].astype(jnp.bfloat16)
    halo = []
    for i in range(2):
        for s in range(strips):
            halo.append(
                pltpu.make_async_remote_copy(
                    edge.at[i],
                    cols_in.at[1 - i, me_s],
                    hsend.at[i, s],
                    hrecv.at[1 - i, me_s],
                    device_id={"strip": s, "tile": sides[i]},
                    device_id_type=MESH,
                )
            )
    for i in range(2):
        halo.append(
            pltpu.make_async_remote_copy(
                image_ref.at[(rows - 1) * (1 - i)],
                rows_in.at[i],
                hsend.at[2, i],
                hrecv.at[2, i],
                device_id={"strip": (me_s + 1 + i * (strips - 2)) % strips, "tile": tile},
                device_id_type=MESH,
            )
        )
    for copy in halo:
        copy.start()

    lanes = 128
    chunks = wexp_ref.shape[1] // lanes
    pad = 8
    group = 4

    def expand(pixels):
        normed = (pixels.astype(jnp.float32) * bng_ref[...] + bns_ref[...]).astype(jnp.bfloat16)
        return gelu_tanh(dot(normed, wexp_ref[...]) + bexp_ref[...])

    @pl.loop(0, rows // group)
    def _(q):
        pixels = image_ref[pl.ds(group * q, group)].reshape(group * cols, chans)
        act = expand(pixels)
        for c in range(chunks):
            e_s[pl.ds(group * q + 1, group), c, pad : pad + cols, :] = act[
                :, lanes * c : lanes * (c + 1)
            ].reshape(group, cols, lanes)

    for i in range(2):
        for s in range(strips):
            pltpu.make_async_copy(cols_in.at[i, s], cols_in.at[i, s], hrecv.at[i, s]).wait()
        pltpu.make_async_copy(rows_in.at[i], rows_in.at[i], hrecv.at[2, i]).wait()
    row_ok = (
        jnp.where(me_s > 0, 1.0, 0.0),
        jnp.where(me_s < strips - 1, 1.0, 0.0),
    )
    col_ok = (
        jnp.where(tile > 0, 1.0, 0.0),
        jnp.where(tile < tiles - 1, 1.0, 0.0),
    )
    for i in range(2):
        act = expand(rows_in[i]) * row_ok[i]
        for c in range(chunks):
            e_s[(rows + 1) * i, c, pad : pad + cols, :] = act[:, lanes * c : lanes * (c + 1)]
        act = expand(cols_in[i].reshape(strips * rows, chans)) * col_ok[i]
        rim[i, 0:8] = jnp.zeros((8, act.shape[1]), jnp.float32)
        rim[i, 8 : 8 + strips * rows] = act
        rim[i, 8 + strips * rows :] = jnp.zeros((8, act.shape[1]), jnp.float32)

    for i in range(2):
        at = (pad + cols) * i

        @pl.loop(0, rows + 2)
        def _(r):
            line = rim[i, pl.ds(me_s * rows + 7 + r, 1), :]
            for c in range(chunks):
                e_s[r, c, at : at + 8, :] = jnp.broadcast_to(
                    line[:, lanes * c : lanes * (c + 1)], (8, lanes)
                )

    def first_copy(s, k, g):
        src = sec_ref.at[g, k, pl.ds(part * s, part)]
        dst = arr.at[grid_rows * me_s + g, me_k]
        return (
            lambda: pltpu.make_async_remote_copy(
                src,
                dst,
                send1.at[s, k],
                recv1.at[me_s, me_k],
                device_id=device(s, k),
                device_id_type=MESH,
            ),
            lambda: pltpu.make_async_copy(src, dst, recv1.at[me_s, me_k]),
        )

    groups = rows // group
    per_grid = groups // grid_rows
    far = (me_k // (GRID // per_grid) + 1) % per_grid

    @pl.loop(0, groups)
    def _(m):
        g = m % grid_rows
        sub = (far + m // grid_rows) % per_grid
        q = per_grid * g + sub
        for c in range(chunks):
            at = slice(lanes * c, lanes * (c + 1))
            acc = [jnp.broadcast_to(bdep_ref[:, at], (cols, lanes))] * group
            for r in range(group + 2):
                for j in range(3):
                    v = e_s[group * q + r, c, pad - 1 + j : pad - 1 + j + cols, :]
                    for o in range(group):
                        if 0 <= r - o <= 2:
                            tap = 3 * (r - o) + j
                            acc[o] = acc[o] + v * wdep_ref[tap : tap + 1, at]
            for o in range(group):
                h_s[cols * o : cols * (o + 1), at] = gelu_tanh(acc[o]).astype(jnp.bfloat16)
        skip = image_ref[pl.ds(group * q, group)].reshape(group * cols, chans).astype(jnp.float32)
        sec = skip + dot(h_s[...], wproj_ref[...]) + bproj_ref[...]
        sec_ref[g, pl.ds(group * sub, group)] = sec.astype(jnp.bfloat16).reshape(
            group, cols, chans
        )
        for r in range(group):
            for s in range(strips):
                k = group * sub + r
                remote, own = first_copy(s, k, g)

                @pl.when(jnp.logical_not(is_me(s, k)))
                def _():
                    remote().start()

                @pl.when(is_me(s, k))
                def _():
                    own().start()

    def wait_first(s, k):
        piece_ref = arr.at[pl.ds(grid_rows * s, grid_rows), k]
        pltpu.make_async_copy(piece_ref, piece_ref, recv1.at[s, k]).wait()

    span = piece * part
    row_id = lax.broadcasted_iota(jnp.int32, (span, span), 0)
    col_id = lax.broadcasted_iota(jnp.int32, (span, span), 1)
    swap = jnp.where(col_id == (row_id % piece) * part + row_id // piece, 1.0, 0.0).astype(
        jnp.bfloat16
    )
    lane_head = lax.broadcasted_iota(jnp.int32, (head_count * piece, chans), 1) // head_size
    row_id = lax.broadcasted_iota(jnp.int32, (head_count * piece, chans), 0)
    row_head = row_id // GRID % head_count
    mask = jnp.where(lane_head == row_head, 1.0, 0.0)
    mask_bf = mask.astype(jnp.bfloat16)

    blocks_per_strip = blocks // strips
    for b in range(blocks):
        if b % blocks_per_strip == 0:
            for k in range(GRID):
                wait_first(b // blocks_per_strip, k)
        x = arr[per_block * b : per_block * (b + 1)].reshape(span, chans).astype(jnp.float32)
        normed = layer_norm(x, ag_ref[...], as_ref[...]).astype(jnp.bfloat16)
        normed = dot(swap, normed).astype(jnp.bfloat16)
        qkv = dot(normed, wqkv_ref[...])
        q = (qkv[:, :chans] * head_size ** (-0.5)).reshape(part, per_block, GRID, chans)
        q_s[b] = jnp.concatenate([q, q], axis=2).astype(jnp.bfloat16)
        k_s[:, piece * b : piece * (b + 1), :] = (
            qkv[:, chans : 2 * chans].astype(jnp.bfloat16).reshape(part, piece, chans)
        )
        v_s[:, piece * b : piece * (b + 1), :] = (
            qkv[:, 2 * chans :].astype(jnp.bfloat16).reshape(part, piece, chans)
        )

    def back_copy(b, k):
        s = b // blocks_per_strip
        half = b % blocks_per_strip
        src = outb.at[pl.ds(per_block * b, per_block), k]
        dst = sec2.at[pl.ds(per_block * half, per_block), me_k, pl.ds(part * me_s, part)]
        return (
            s,
            lambda: pltpu.make_async_remote_copy(
                src,
                dst,
                send2.at[b, k],
                recv2.at[half, me_s, me_k],
                device_id=device(s, k),
                device_id_type=MESH,
            ),
            lambda: pltpu.make_async_copy(src, dst, recv2.at[half, me_s, me_k]),
        )

    for b in range(blocks):
        bias = jnp.concatenate(
            [bias_ref[GRID - 1 + per_block * b - k] for k in range(GRID)], axis=0
        )
        for w in range(part):
            qbd = (
                jnp.concatenate(
                    [q_s[b, w, i] for i in range(per_block) for _ in range(head_count // 2)], axis=0
                )
                * mask_bf
            )
            s = lax.dot_general(
                k_s[w], qbd, (((1,), (1,)), ((), ())), preferred_element_type=jnp.float32
            )
            s = s + bias
            e = jnp.exp(s - jnp.max(s, axis=0, keepdims=True))
            p = (e * (1.0 / jnp.sum(e, axis=0, keepdims=True))).astype(jnp.bfloat16)
            o = lax.dot_general(
                p, v_s[w], (((0,), (0,)), ((), ())), preferred_element_type=jnp.float32
            )
            o = (o * mask).reshape(per_block, head_count, GRID, chans)
            ctx_s[w] = jnp.sum(o, axis=1).reshape(piece, chans).astype(jnp.bfloat16)
        ctx = dot(swap, ctx_s[...].reshape(span, chans)).astype(jnp.bfloat16)
        x = arr[per_block * b : per_block * (b + 1)].reshape(span, chans).astype(jnp.float32)
        attended = (x + dot(ctx, wout_ref[...])).astype(jnp.bfloat16)
        outb[per_block * b : per_block * (b + 1)] = attended.reshape(per_block, GRID, part, chans)
        for m in range(GRID):
            k = (me_k + m) % GRID
            s, remote, own = back_copy(b, k)

            @pl.when(jnp.logical_not(is_me(s, k)))
            def _():
                remote().start()

            @pl.when(is_me(s, k))
            def _():
                own().start()

    pairs = GRID // 2
    for m in range(pairs):
        pair = (me_k // 2 + m) % pairs
        for s in range(strips):
            for kk in range(2):
                k = 2 * pair + kk
                for half in range(blocks_per_strip):
                    ref = sec2.at[pl.ds(per_block * half, per_block), k, pl.ds(part * s, part)]
                    pltpu.make_async_copy(ref, ref, recv2.at[half, s, k]).wait()
        x = sec2[:, pl.ds(2 * pair, 2)].reshape(grid_rows * 2 * cols, chans).astype(jnp.float32)
        normed = layer_norm(x, fg_ref[...], fs_ref[...]).astype(jnp.bfloat16)
        hidden = gelu_tanh(dot(normed, wup_ref[...]) + bup_ref[...]).astype(jnp.bfloat16)
        res = x + dot(hidden, wdown_ref[...]) + bdown_ref[...]
        out_ref[:, pl.ds(2 * pair, 2)] = res.reshape(grid_rows, 2, cols, chans)

    for copy in halo:
        copy.wait_send()
    for s in range(strips):
        for k in range(GRID):

            @pl.when(jnp.logical_not(is_me(s, k)))
            def _():
                src = sec_ref.at[:, k, pl.ds(part * s, part)]
                dst = arr.at[pl.ds(grid_rows * me_s, grid_rows), me_k]
                pltpu.make_async_remote_copy(
                    src,
                    dst,
                    send1.at[s, k],
                    recv1.at[me_s, me_k],
                    device_id=device(s, k),
                    device_id_type=MESH,
                ).wait_send()

    for b in range(blocks):
        for k in range(GRID):
            s, remote, own = back_copy(b, k)

            @pl.when(jnp.logical_not(is_me(s, k)))
            def _():
                remote().wait_send()


def local(
    image,
    bn_gain,
    bn_shift,
    w_expand,
    b_expand,
    w_depth,
    b_depth,
    w_project,
    b_project,
    attn_gain,
    attn_shift,
    w_qkv,
    w_out,
    rel_table,
    ffn_gain,
    ffn_shift,
    w_up,
    b_up,
    w_down,
    b_down,
):
    tile_rows, tile_cols, channels = image.shape
    strips = lax.axis_size("strip")
    tile_count = lax.axis_size("tile")
    grid_rows = GRID // strips
    across = tile_rows // grid_rows
    col_groups = tile_count // GRID
    heads = rel_table.shape[0]
    part = tile_cols // strips
    piece = part
    blocks = GRID * GRID // piece
    bias = place_bias(rel_table)
    hidden = w_expand.shape[1]
    bf, f32 = jnp.bfloat16, jnp.float32
    vmem = pl.BlockSpec(memory_space=pltpu.VMEM)
    out = pl.pallas_call(
        functools.partial(block_kernel, strips, col_groups, heads),
        out_shape=jax.ShapeDtypeStruct((grid_rows, across, tile_cols, channels), f32),
        in_specs=[vmem] * 20,
        out_specs=vmem,
        scratch_shapes=[
            pltpu.VMEM((2, tile_rows, channels), bf),
            pltpu.VMEM((2, strips, tile_rows, channels), bf),
            pltpu.VMEM((2, tile_cols, channels), bf),
            pltpu.VMEM((2, strips * tile_rows + 16, hidden), f32),
            pltpu.VMEM((tile_rows + 2, hidden // 128, tile_cols + 16, 128), f32),
            pltpu.VMEM((4 * tile_cols, hidden), bf),
            pltpu.VMEM((grid_rows, across, tile_cols, channels), bf),
            pltpu.VMEM((GRID, GRID, part, channels), bf),
            pltpu.VMEM((blocks, part, piece // GRID, 2 * GRID, channels), bf),
            pltpu.VMEM((part, GRID * GRID, channels), bf),
            pltpu.VMEM((part, GRID * GRID, channels), bf),
            pltpu.VMEM((part, piece, channels), bf),
            pltpu.VMEM((GRID, GRID, part, channels), bf),
            pltpu.VMEM((grid_rows, GRID, tile_cols, channels), bf),
            pltpu.SemaphoreType.DMA((strips, GRID)),
            pltpu.SemaphoreType.DMA((strips, GRID)),
            pltpu.SemaphoreType.DMA((blocks, GRID)),
            pltpu.SemaphoreType.DMA((blocks // strips, strips, GRID)),
            pltpu.SemaphoreType.DMA((3, 2)),
            pltpu.SemaphoreType.DMA((3, 2)),
        ],
        compiler_params=pltpu.CompilerParams(collective_id=0, has_side_effects=True),
    )(
        image,
        bn_gain.reshape(1, -1),
        bn_shift.reshape(1, -1),
        w_expand,
        b_expand.reshape(1, -1),
        w_depth,
        b_depth.reshape(1, -1),
        w_project,
        b_project.reshape(1, -1),
        attn_gain.reshape(1, -1),
        attn_shift.reshape(1, -1),
        w_qkv,
        w_out,
        bias,
        ffn_gain.reshape(1, -1),
        ffn_shift.reshape(1, -1),
        w_up,
        b_up.reshape(1, -1),
        w_down,
        b_down.reshape(1, -1),
    )
    return out.astype(bf).reshape(tile_rows, tile_cols, channels)


def solution(mesh):
    return jax.shard_map(
        local,
        mesh=mesh,
        in_specs=(P(("group", "strip"), "tile", None),) + (P(),) * 19,
        out_specs=P(("group", "strip"), "tile", None),
        check_vma=False,
    )
```

```python
import functools

import jax
import jax.numpy as jnp
from jax import lax
from jax.experimental import pallas as pl
from jax.experimental.pallas import tpu as pltpu
from jax.sharding import PartitionSpec as P

GRID = 8
EPSILON = 1e-05
MESH = pl.DeviceIdType.MESH
ORDER = (4, 5, 3, 2, 6, 1, 7, 0)


def gelu_tanh(inputs):
    return jax.nn.gelu(inputs, approximate=True)


def layer_norm(inputs, norm_gain, norm_shift):
    center = jnp.mean(inputs, axis=-1, keepdims=True)
    spread = jnp.mean(jnp.square(inputs - center), axis=-1, keepdims=True)
    return (inputs - center) * lax.rsqrt(spread + EPSILON) * norm_gain + norm_shift


def place_bias(rel_table):
    heads = rel_table.shape[0]
    side = 2 * GRID - 1
    table = rel_table.reshape(heads, side, side)
    shape = (side, GRID, GRID)
    entry = lax.broadcasted_iota(jnp.int32, shape, 0)
    key = lax.broadcasted_iota(jnp.int32, shape, 1)
    query = lax.broadcasted_iota(jnp.int32, shape, 2)
    onehot = (entry == GRID - 1 + query - key).astype(jnp.float32)
    by_col = jnp.einsum("hde,eki->dkhi", table, onehot, precision=lax.Precision.HIGHEST)
    by_col = by_col.reshape(side, GRID, heads * GRID)
    return jnp.concatenate([by_col[:-1], by_col[1:]], axis=-1)


def dot(a, b):
    return jnp.dot(a, b, preferred_element_type=jnp.float32)


def block_kernel(
    strips,
    col_groups,
    head_count,
    image_ref,
    bng_ref,
    bns_ref,
    wexp_ref,
    bexp_ref,
    wdep_ref,
    bdep_ref,
    wproj_ref,
    bproj_ref,
    ag_ref,
    as_ref,
    wqkv_ref,
    wout_ref,
    bias_ref,
    fg_ref,
    fs_ref,
    wup_ref,
    bup_ref,
    wdown_ref,
    bdown_ref,
    out_ref,
    edge,
    cols_in,
    rows_in,
    rim,
    e_s,
    h_s,
    sec_ref,
    arr,
    q_s,
    k_s,
    v_s,
    ctx_s,
    outb,
    sec2,
    send1,
    recv1,
    send2,
    recv2,
    hsend,
    hrecv,
):
    grid_rows, _, cols, chans = sec_ref.shape
    part = cols // strips
    rows = image_ref.shape[0]
    piece = ctx_s.shape[1]
    blocks = GRID * GRID // piece
    per_block = piece // GRID
    head_size = chans // head_count
    me_s = lax.axis_index("strip")
    tile = lax.axis_index("tile")
    me_k = tile // col_groups
    within = tile % col_groups
    peers = strips * GRID

    def device(s, k):
        return {"strip": s, "tile": k * col_groups + within}

    def is_me(s, k):
        return jnp.logical_and(s == me_s, k == me_k)

    barrier = pltpu.get_barrier_semaphore()
    for m in range(1, peers):
        s, k = (me_s + m // GRID) % strips, (me_k + m) % GRID
        pl.semaphore_signal(barrier, inc=1, device_id=device(s, k), device_id_type=MESH)
    tiles = GRID * col_groups
    sides = ((tile + tiles - 1) % tiles, (tile + 1) % tiles)
    for t in sides:
        for s in range(strips):
            pl.semaphore_signal(
                barrier, inc=1, device_id={"strip": s, "tile": t}, device_id_type=MESH
            )
    pl.semaphore_wait(barrier, peers - 1 + 2 * strips)

    edge[0] = image_ref[:, 0:16, :].astype(jnp.float32)[:, 0, :].astype(jnp.bfloat16)
    edge[1] = image_ref[:, cols - 16 : cols, :].astype(jnp.float32)[:, 15, :].astype(jnp.bfloat16)
    halo = []
    for i in range(2):
        for s in range(strips):
            halo.append(
                pltpu.make_async_remote_copy(
                    edge.at[i],
                    cols_in.at[1 - i, me_s],
                    hsend.at[i, s],
                    hrecv.at[1 - i, me_s],
                    device_id={"strip": s, "tile": sides[i]},
                    device_id_type=MESH,
                )
            )
    for i in range(2):
        halo.append(
            pltpu.make_async_remote_copy(
                image_ref.at[(rows - 1) * (1 - i)],
                rows_in.at[i],
                hsend.at[2, i],
                hrecv.at[2, i],
                device_id={"strip": (me_s + 1 + i * (strips - 2)) % strips, "tile": tile},
                device_id_type=MESH,
            )
        )
    for copy in halo:
        copy.start()

    lanes = 128
    chunks = wexp_ref.shape[1] // lanes
    pad = 8
    group = 4

    def expand(pixels):
        normed = (pixels.astype(jnp.float32) * bng_ref[...] + bns_ref[...]).astype(jnp.bfloat16)
        return gelu_tanh(dot(normed, wexp_ref[...]) + bexp_ref[...])

    groups = rows // group
    ahead = 3

    def expand_rows(q):
        pixels = image_ref[pl.ds(group * q, group)].reshape(group * cols, chans)
        act = expand(pixels)
        for c in range(chunks):
            e_s[pl.ds(group * q + 1, group), c, pad : pad + cols, :] = act[
                :, lanes * c : lanes * (c + 1)
            ].reshape(group, cols, lanes)

    @pl.loop(0, ahead)
    def _(q):
        expand_rows(q)

    for i in range(2):
        for s in range(strips):
            pltpu.make_async_copy(cols_in.at[i, s], cols_in.at[i, s], hrecv.at[i, s]).wait()
        pltpu.make_async_copy(rows_in.at[i], rows_in.at[i], hrecv.at[2, i]).wait()
    row_ok = (
        jnp.where(me_s > 0, 1.0, 0.0),
        jnp.where(me_s < strips - 1, 1.0, 0.0),
    )
    col_ok = (
        jnp.where(tile > 0, 1.0, 0.0),
        jnp.where(tile < tiles - 1, 1.0, 0.0),
    )
    for i in range(2):
        act = expand(rows_in[i]) * row_ok[i]
        for c in range(chunks):
            e_s[(rows + 1) * i, c, pad : pad + cols, :] = act[:, lanes * c : lanes * (c + 1)]
        act = expand(cols_in[i].reshape(strips * rows, chans)) * col_ok[i]
        rim[i, 0:8] = jnp.zeros((8, act.shape[1]), jnp.float32)
        rim[i, 8 : 8 + strips * rows] = act
        rim[i, 8 + strips * rows :] = jnp.zeros((8, act.shape[1]), jnp.float32)

    for i in range(2):
        at = (pad + cols) * i

        @pl.loop(0, rows + 2)
        def _(r):
            line = rim[i, pl.ds(me_s * rows + 7 + r, 1), :]
            for c in range(chunks):
                e_s[r, c, at : at + 8, :] = jnp.broadcast_to(
                    line[:, lanes * c : lanes * (c + 1)], (8, lanes)
                )

    def first_copy(s, k, g):
        src = sec_ref.at[g, k, pl.ds(part * s, part)]
        dst = arr.at[grid_rows * me_s + g, me_k]
        return (
            lambda: pltpu.make_async_remote_copy(
                src,
                dst,
                send1.at[s, k],
                recv1.at[me_s, me_k],
                device_id=device(s, k),
                device_id_type=MESH,
            ),
            lambda: pltpu.make_async_copy(src, dst, recv1.at[me_s, me_k]),
        )

    per_grid = groups // grid_rows

    @pl.loop(0, groups)
    def _(q):
        @pl.when(q + ahead < groups)
        def _():
            expand_rows(q + ahead)

        g = q // per_grid
        sub = q % per_grid
        for c in range(chunks):
            at = slice(lanes * c, lanes * (c + 1))
            acc = [jnp.broadcast_to(bdep_ref[:, at], (cols, lanes))] * group
            for r in range(group + 2):
                for j in range(3):
                    v = e_s[group * q + r, c, pad - 1 + j : pad - 1 + j + cols, :]
                    for o in range(group):
                        if 0 <= r - o <= 2:
                            tap = 3 * (r - o) + j
                            acc[o] = acc[o] + v * wdep_ref[tap : tap + 1, at]
            for o in range(group):
                h_s[cols * o : cols * (o + 1), at] = gelu_tanh(acc[o]).astype(jnp.bfloat16)
        skip = image_ref[pl.ds(group * q, group)].reshape(group * cols, chans).astype(jnp.float32)
        sec = skip + dot(h_s[...], wproj_ref[...]) + bproj_ref[...]
        sec_ref[g, pl.ds(group * sub, group)] = sec.astype(jnp.bfloat16).reshape(
            group, cols, chans
        )
        for r in range(group):
            for s in range(strips):
                k = group * sub + r
                remote, own = first_copy(s, k, g)

                @pl.when(jnp.logical_not(is_me(s, k)))
                def _():
                    remote().start()

                @pl.when(is_me(s, k))
                def _():
                    own().start()

    def wait_first(s, k):
        piece_ref = arr.at[pl.ds(grid_rows * s, grid_rows), k]
        pltpu.make_async_copy(piece_ref, piece_ref, recv1.at[s, k]).wait()

    span = piece * part
    row_id = lax.broadcasted_iota(jnp.int32, (span, span), 0)
    col_id = lax.broadcasted_iota(jnp.int32, (span, span), 1)
    swap = jnp.where(col_id == (row_id % piece) * part + row_id // piece, 1.0, 0.0).astype(
        jnp.bfloat16
    )
    lane_head = lax.broadcasted_iota(jnp.int32, (head_count * piece, chans), 1) // head_size
    row_id = lax.broadcasted_iota(jnp.int32, (head_count * piece, chans), 0)
    row_head = row_id // GRID % head_count
    mask = jnp.where(lane_head == row_head, 1.0, 0.0)
    mask_bf = mask.astype(jnp.bfloat16)

    blocks_per_strip = blocks // strips
    for b in range(blocks):
        if b % blocks_per_strip == 0:
            for k in range(GRID):
                wait_first(b // blocks_per_strip, k)
        x = arr[per_block * b : per_block * (b + 1)].reshape(span, chans).astype(jnp.float32)
        normed = layer_norm(x, ag_ref[...], as_ref[...]).astype(jnp.bfloat16)
        normed = dot(swap, normed).astype(jnp.bfloat16)
        qkv = dot(normed, wqkv_ref[...])
        q = (qkv[:, :chans] * head_size ** (-0.5)).reshape(part, per_block, GRID, chans)
        q_s[b] = jnp.concatenate([q, q], axis=2).astype(jnp.bfloat16)
        k_s[:, piece * b : piece * (b + 1), :] = (
            qkv[:, chans : 2 * chans].astype(jnp.bfloat16).reshape(part, piece, chans)
        )
        v_s[:, piece * b : piece * (b + 1), :] = (
            qkv[:, 2 * chans :].astype(jnp.bfloat16).reshape(part, piece, chans)
        )

    def block_of(i):
        s = (me_s + 1 + i % strips) % strips
        half = i // strips
        return s, half, blocks_per_strip * s + half

    def back_copy(i, k):
        s, half, b = block_of(i)
        src = outb.at[pl.ds(per_block * b, per_block), k]
        dst = sec2.at[pl.ds(per_block * half, per_block), me_k, pl.ds(part * me_s, part)]
        return (
            s,
            lambda: pltpu.make_async_remote_copy(
                src,
                dst,
                send2.at[i, k],
                recv2.at[half, me_s, me_k],
                device_id=device(s, k),
                device_id_type=MESH,
            ),
            lambda: pltpu.make_async_copy(src, dst, recv2.at[half, me_s, me_k]),
        )

    for i in range(blocks):
        b = block_of(i)[2]
        bias = jnp.concatenate(
            [bias_ref[GRID - 1 + per_block * b - k] for k in range(GRID)], axis=0
        )
        for w in range(part):
            qbd = (
                jnp.concatenate(
                    [q_s[b, w, j] for j in range(per_block) for _ in range(head_count // 2)], axis=0
                )
                * mask_bf
            )
            s = lax.dot_general(
                k_s[w], qbd, (((1,), (1,)), ((), ())), preferred_element_type=jnp.float32
            )
            s = s + bias
            e = jnp.exp(s - jnp.max(s, axis=0, keepdims=True))
            p = (e * (1.0 / jnp.sum(e, axis=0, keepdims=True))).astype(jnp.bfloat16)
            o = lax.dot_general(
                p, v_s[w], (((0,), (0,)), ((), ())), preferred_element_type=jnp.float32
            )
            o = (o * mask).reshape(per_block, head_count, GRID, chans)
            ctx_s[w] = jnp.sum(o, axis=1).reshape(piece, chans).astype(jnp.bfloat16)
        ctx = dot(swap, ctx_s[...].reshape(span, chans)).astype(jnp.bfloat16)
        x = arr[pl.ds(per_block * b, per_block)].reshape(span, chans).astype(jnp.float32)
        attended = (x + dot(ctx, wout_ref[...])).astype(jnp.bfloat16)
        outb[pl.ds(per_block * b, per_block)] = attended.reshape(per_block, GRID, part, chans)
        for m in ORDER:
            k = (me_k + m) % GRID
            s, remote, own = back_copy(i, k)

            @pl.when(jnp.logical_not(is_me(s, k)))
            def _():
                remote().start()

            @pl.when(is_me(s, k))
            def _():
                own().start()

    pairs = GRID // 2
    for m in range(pairs):
        pair = (me_k // 2 + m) % pairs
        for s in range(strips):
            for kk in range(2):
                k = 2 * pair + kk
                for half in range(blocks_per_strip):
                    ref = sec2.at[pl.ds(per_block * half, per_block), k, pl.ds(part * s, part)]
                    pltpu.make_async_copy(ref, ref, recv2.at[half, s, k]).wait()
        x = sec2[:, pl.ds(2 * pair, 2)].reshape(grid_rows * 2 * cols, chans).astype(jnp.float32)
        normed = layer_norm(x, fg_ref[...], fs_ref[...]).astype(jnp.bfloat16)
        hidden = gelu_tanh(dot(normed, wup_ref[...]) + bup_ref[...]).astype(jnp.bfloat16)
        res = x + dot(hidden, wdown_ref[...]) + bdown_ref[...]
        out_ref[:, pl.ds(2 * pair, 2)] = res.reshape(grid_rows, 2, cols, chans)

    for copy in halo:
        copy.wait_send()
    for s in range(strips):
        for k in range(GRID):

            @pl.when(jnp.logical_not(is_me(s, k)))
            def _():
                src = sec_ref.at[:, k, pl.ds(part * s, part)]
                dst = arr.at[pl.ds(grid_rows * me_s, grid_rows), me_k]
                pltpu.make_async_remote_copy(
                    src,
                    dst,
                    send1.at[s, k],
                    recv1.at[me_s, me_k],
                    device_id=device(s, k),
                    device_id_type=MESH,
                ).wait_send()

    for i in range(blocks):
        for k in range(GRID):
            s, remote, own = back_copy(i, k)

            @pl.when(jnp.logical_not(is_me(s, k)))
            def _():
                remote().wait_send()


def local(
    image,
    bn_gain,
    bn_shift,
    w_expand,
    b_expand,
    w_depth,
    b_depth,
    w_project,
    b_project,
    attn_gain,
    attn_shift,
    w_qkv,
    w_out,
    rel_table,
    ffn_gain,
    ffn_shift,
    w_up,
    b_up,
    w_down,
    b_down,
):
    tile_rows, tile_cols, channels = image.shape
    strips = lax.axis_size("strip")
    tile_count = lax.axis_size("tile")
    grid_rows = GRID // strips
    across = tile_rows // grid_rows
    col_groups = tile_count // GRID
    heads = rel_table.shape[0]
    part = tile_cols // strips
    piece = part
    blocks = GRID * GRID // piece
    bias = place_bias(rel_table)
    hidden = w_expand.shape[1]
    bf, f32 = jnp.bfloat16, jnp.float32
    vmem = pl.BlockSpec(memory_space=pltpu.VMEM)
    out = pl.pallas_call(
        functools.partial(block_kernel, strips, col_groups, heads),
        out_shape=jax.ShapeDtypeStruct((grid_rows, across, tile_cols, channels), f32),
        in_specs=[vmem] * 20,
        out_specs=vmem,
        scratch_shapes=[
            pltpu.VMEM((2, tile_rows, channels), bf),
            pltpu.VMEM((2, strips, tile_rows, channels), bf),
            pltpu.VMEM((2, tile_cols, channels), bf),
            pltpu.VMEM((2, strips * tile_rows + 16, hidden), f32),
            pltpu.VMEM((tile_rows + 2, hidden // 128, tile_cols + 16, 128), f32),
            pltpu.VMEM((4 * tile_cols, hidden), bf),
            pltpu.VMEM((grid_rows, across, tile_cols, channels), bf),
            pltpu.VMEM((GRID, GRID, part, channels), bf),
            pltpu.VMEM((blocks, part, piece // GRID, 2 * GRID, channels), bf),
            pltpu.VMEM((part, GRID * GRID, channels), bf),
            pltpu.VMEM((part, GRID * GRID, channels), bf),
            pltpu.VMEM((part, piece, channels), bf),
            pltpu.VMEM((GRID, GRID, part, channels), bf),
            pltpu.VMEM((grid_rows, GRID, tile_cols, channels), bf),
            pltpu.SemaphoreType.DMA((strips, GRID)),
            pltpu.SemaphoreType.DMA((strips, GRID)),
            pltpu.SemaphoreType.DMA((blocks, GRID)),
            pltpu.SemaphoreType.DMA((blocks // strips, strips, GRID)),
            pltpu.SemaphoreType.DMA((3, 2)),
            pltpu.SemaphoreType.DMA((3, 2)),
        ],
        compiler_params=pltpu.CompilerParams(
            collective_id=0, has_side_effects=True, vmem_limit_bytes=24 * 2**20
        ),
    )(
        image,
        bn_gain.reshape(1, -1),
        bn_shift.reshape(1, -1),
        w_expand,
        b_expand.reshape(1, -1),
        w_depth,
        b_depth.reshape(1, -1),
        w_project,
        b_project.reshape(1, -1),
        attn_gain.reshape(1, -1),
        attn_shift.reshape(1, -1),
        w_qkv,
        w_out,
        bias,
        ffn_gain.reshape(1, -1),
        ffn_shift.reshape(1, -1),
        w_up,
        b_up.reshape(1, -1),
        w_down,
        b_down.reshape(1, -1),
    )
    return out.astype(bf).reshape(tile_rows, tile_cols, channels)


def solution(mesh):
    return jax.shard_map(
        local,
        mesh=mesh,
        in_specs=(P(("group", "strip"), "tile", None),) + (P(),) * 19,
        out_specs=P(("group", "strip"), "tile", None),
        check_vma=False,
    )
```
